32 devices in a mesh: row: 4 (over x, core), col: 8 (over z, y).
Axes of the slice: x: 2, y: 2, z: 4, core: 2. Of those that a mesh axis runs over, the one named last changes fastest.
Arguments:
- vectors: float32 [512, 4096], P('row', 'col'), may hold values from -6 to 6
- factors: float32 [8, 4, 512, 512], P('col', None, 'row'), may hold values from -1 to 1, as said below
- offsets: int32 [8], replicated, may hold values from 0 to 1
Outputs:
- updated: float32 [512, 4096], P('row', 'col')
The draws below stay inside these ranges and needn't reach their ends.
Inputs may be any that keep to these rules, and one draw needn't show every extreme that they name: Each factors[c, k] is an orthogonal matrix.
All inputs are finite; a program needn't handle non-finite values.
Results may differ from the reference program's by a relative error of at most 0.00014.
Values sent between devices are 32-bit elements; how exact they have to be, the bound alone decides.
No kernel may reach another device: no remote copies, remote signals or barrier semaphores. Data moves between devices by JAX's collectives and lax.ppermute only.
A program may use at most 64 MiB of HBM per device.

```python
import jax
import jax.numpy as jnp
from jax import lax

F = 512
NROWS = 512
WIN = 4096
CHAINS = 8


def draw_factors(key, part):
    sample = jax.random.normal(key, (CHAINS * 4, F, F), jnp.float32)
    orthogonal, upper_tri = jnp.linalg.qr(sample)
    return orthogonal.reshape(CHAINS, 4, F, F)


def plant(array, key, least, high):
    longest = array.shape.index(max(array.shape))
    spots = []
    for shift in (0, 1):
        where = [jax.random.randint(jax.random.fold_in(key, axis), (), 0, length) for axis, length in enumerate(array.shape)]
        where[longest] = (where[longest] + shift) % array.shape[longest]
        spots.append(tuple(where))
    return array.at[spots[0]].set(least).at[spots[1]].set(high)


def block_levels(own_key, extent, shards, smallest, top_value):
    def one(position, shards_of):
        heights = jax.random.uniform(jax.random.fold_in(jax.random.fold_in(own_key, 6), position), (shards_of,), jnp.float32, smallest / len(shards), top_value / len(shards))
        return jnp.repeat(jnp.exp(heights), extent[position] // shards_of).reshape((-1,) + (1,) * (len(extent) - position - 1))

    loudness = one(*shards[0])
    for cut in shards[1:]:
        loudness = loudness * one(*cut)
    return loudness


def bell_draw(stream_key, shape, deviation, reach, cuts=(), held_as=jnp.bfloat16):
    result = deviation * jax.random.normal(stream_key, shape, jnp.float32)
    if cuts:
        result = result * block_levels(stream_key, shape, cuts, -0.22, 0.18)
    return jnp.clip(result, -reach, reach).astype(held_as)


def setup_inputs(seed: int = 0) -> dict:
    key_list = jax.random.split(jax.random.key(seed), 4)
    return {
        "vectors": bell_draw(key_list[0], (NROWS, WIN), 1.0, 6.0, ((0, 4), (1, 8)), jnp.float32),
        "factors": draw_factors(jax.random.fold_in(key_list[3], 71), 0),
        "offsets": plant(jax.random.randint(key_list[2], (CHAINS,), 0, 2), jax.random.fold_in(key_list[2], 1), 0, 1).astype(jnp.int32),
    }


def apply_chain(section, chain_factors, stride, first_col, width):
    identity = jnp.eye(2 * stride, dtype=jnp.float32)
    for factor_no in range(4):
        valid = first_col + factor_no * stride + 2 * stride <= width
        factor = jnp.where(valid, chain_factors[factor_no], identity)
        before = section[:, :factor_no * stride]
        middle = section[:, factor_no * stride:factor_no * stride + 2 * stride]
        beyond = section[:, factor_no * stride + 2 * stride:]
        middle = jnp.dot(middle.astype(jnp.float32), factor.astype(jnp.float32), precision=lax.Precision.HIGHEST, preferred_element_type=jnp.float32)
        section = jnp.concatenate([before, middle, beyond], 1)
    return section

def reference(vectors, factors, offsets):
    stride = F // 2
    width = vectors.shape[1]
    updated = jnp.concatenate([vectors, jnp.zeros((vectors.shape[0], 4 * stride), jnp.float32)], 1)
    for tick_num in range(3):
        for chain_no in range(tick_num, CHAINS, 3):
            first_col = (chain_no * F + offsets[chain_no] * stride).astype(jnp.int32)
            section = lax.dynamic_slice_in_dim(updated, first_col, 5 * stride, 1)
            section = apply_chain(section, factors[chain_no], stride, first_col, width)
            updated = lax.dynamic_update_slice_in_dim(updated, section, first_col, 1)
    return updated[:, :width]
```

```python
import functools

import jax
import jax.numpy as jnp
from jax import lax
from jax.experimental import pallas as pl
from jax.experimental.pallas import tpu as pltpu
from jax.sharding import PartitionSpec as P


FACTORS = 4
TICKS = 3


def split_halves(value):
    high = value.astype(jnp.bfloat16)
    low = (value - high.astype(jnp.float32)).astype(jnp.bfloat16)
    return high, low


def product(former, high_ref, low_ref):
    rows = former.shape[0]
    high, low = split_halves(former)
    both = jnp.concatenate([high, low], 0)
    first = jnp.dot(both, high_ref[...], preferred_element_type=jnp.float32)
    second = jnp.dot(high, low_ref[...], preferred_element_type=jnp.float32)
    return first[:rows] + (first[rows:] + second)


def place(groups, offsets_ref):
    column = lax.axis_index("col")
    offset = offsets_ref[column]
    last = 2 * groups - 2 - 2 * column - offset
    return column, lax.rem(column, TICKS), offset, last


def convert(pieces, high_ref, low_ref):
    height = pieces[0].shape[0]
    row = lax.axis_index("row")
    for mask, piece in enumerate(pieces):
        high, low = split_halves(piece[...])
        start = pl.multiple_of((row ^ mask) * height, height)
        high_ref[pl.ds(start, height), :] = high
        low_ref[pl.ds(start, height), :] = low


def strips(first, count, stride):
    return (slice(None), pl.ds(pl.multiple_of(first * stride, stride), count * stride))


def early_kernel(groups, ring, numbers, stride, *refs):
    count = len(numbers)
    refs = list(refs)
    offsets_ref = refs.pop(0)
    shift = numbers[0]
    blocks = [refs.pop(0) for _ in range(3 if shift == 0 else 1)]
    pieces = [refs.pop(0) for _ in range(count * ring)]
    results = [refs.pop(0) for _ in range(1 if numbers[-1] == FACTORS - 1 else 2)]
    kept = [refs.pop(0) for _ in range(2 * count)]
    (buf,) = refs
    _, tick, offset, last = place(groups, offsets_ref)
    active = tick == 0

    @pl.when(active)
    def _():
        width = blocks[0].shape[1]
        for i, block in enumerate(blocks):
            buf[:, i * width : (i + 1) * width] = block[...]

    for i, number in enumerate(numbers):
        convert(pieces[i * ring : (i + 1) * ring], kept[2 * i], kept[2 * i + 1])

        @pl.when(active & (number <= last))
        def _():
            begin = 0 if shift == 3 else offset + number - shift
            here = strips(begin, 2, stride)
            buf[here] = product(buf[here], kept[2 * i], kept[2 * i + 1])

    @pl.when(active)
    def _():
        if shift == 0:
            results[0][...] = buf[:, : 2 * stride]
            results[1][...] = buf[:, 2 * stride :]
        elif shift == 2:
            results[0][:, :stride] = buf[:, :stride]
            results[0][:, stride:] = buf[strips(3 - 2 * offset, 1, stride)]
            results[1][...] = buf[strips(1 + offset, 2, stride)]
        else:
            results[0][...] = buf[...]


def late_kernel(groups, when, stride, *refs):
    offsets_ref, outer, final, third = refs[:4]
    weights = refs[4 : 4 + 2 * FACTORS]
    results = refs[4 + 2 * FACTORS : 7 + 2 * FACTORS]
    (buf,) = refs[7 + 2 * FACTORS :]
    column, tick, offset, last = place(groups, offsets_ref)
    before = offsets_ref[jnp.maximum(column - 1, 0)]

    @pl.when(tick == when)
    def _():
        buf[:, :stride] = outer[:, :stride]
        buf[strips(3 - 2 * before, 1, stride)] = outer[:, stride:]
        buf[strips(1 + before, 2, stride)] = final[...]
        buf[:, 4 * stride :] = third[...]
        for number in range(FACTORS):

            @pl.when(number <= last)
            def _():
                here = strips(offset + number, 2, stride)
                buf[here] = product(buf[here], weights[2 * number], weights[2 * number + 1])

        results[0][...] = buf[:, : 2 * stride]
        if when == TICKS - 1:
            results[1][...] = buf[:, 2 * stride : 4 * stride]
            results[2][...] = buf[:, 4 * stride :]
        else:
            results[1][:, :stride] = buf[:, 2 * stride : 3 * stride]
            results[1][:, stride:] = buf[strips(5 - 2 * offset, 1, stride)]
            results[2][...] = buf[strips(3 + offset, 2, stride)]


def pick_kernel(own0, own1, own2, near, far, out):
    column = lax.axis_index("col")
    tick = lax.rem(column, TICKS)
    for source, chosen in (
        (own0, (tick == 0) & (column < TICKS)),
        (near, (tick == 0) & (column >= TICKS)),
        (own1, (tick == 1) & (column < TICKS)),
        (far, (tick == 1) & (column >= TICKS)),
        (own2, tick == 2),
    ):

        @pl.when(chosen)
        def _():
            out[...] = source[...]


def on_device(groups, ring, vectors, factors, offsets):
    rows, width = vectors.shape
    stride = width // 2
    height = factors.shape[2]
    order = ring * height
    f32, bf16 = jnp.float32, jnp.bfloat16
    on_chip = pl.BlockSpec(memory_space=pltpu.VMEM)
    scalars = pl.BlockSpec(memory_space=pltpu.SMEM)
    bits = [1 << i for i in range(ring.bit_length() - 1)][::-1]

    def along(array, distance, tick):
        pairs = [
            (i, i + distance)
            for i in range(groups)
            if i % TICKS == tick and 0 <= i + distance < groups
        ]
        return lax.ppermute(array, "col", pairs)

    def swapped(array, bit):
        return lax.ppermute(array, "row", [(i, i ^ bit) for i in range(ring)])

    def call(kernel, outs, scratch, *operands):
        return pl.pallas_call(
            kernel,
            out_shape=outs,
            in_specs=[scalars if op.dtype == jnp.int32 else on_chip for op in operands],
            out_specs=[on_chip] * len(outs),
            scratch_shapes=scratch,
            compiler_params=pltpu.CompilerParams(vmem_limit_bytes=24 << 20),
        )(*operands)

    def block(columns=width, dtype=f32, high=rows):
        return jax.ShapeDtypeStruct((high, columns), dtype)

    gathered = []
    for number in range(FACTORS):
        pieces = {0: factors[0, number]}
        for bit in bits:
            for mask in list(pieces):
                pieces[mask ^ bit] = swapped(pieces[mask], bit)
        gathered.append([pieces[mask] for mask in range(ring)])

    beside = along(vectors, -1, 1)
    distant = along(vectors, -2, 2)

    def early(numbers, blocks, outs):
        count = len(numbers)
        kept = [block(order, bf16, order)] * (2 * count)
        span = sum(b.shape[1] for b in blocks)
        scratch = [pltpu.VMEM((rows, span), f32)]
        pieces = [piece for number in numbers for piece in gathered[number]]
        results = call(
            functools.partial(early_kernel, groups, ring, numbers, stride),
            outs + kept,
            scratch,
            offsets,
            *blocks,
            *pieces,
        )
        return results[: len(outs)], results[len(outs) :]

    (own0, rest), kept01 = early((0, 1), [vectors, beside, distant], [block(), block(2 * width)])
    third = along(own0, -2, 0)
    (outer, passing), kept2 = early((2,), [rest], [block(), block()])
    outer = along(outer, 1, 0)
    (final,), kept3 = early((3,), [passing], [block()])
    final = along(final, 1, 0)
    weights = [*kept01, *kept2, *kept3]

    def late(when, outer, final, third):
        scratch = [pltpu.VMEM((rows, 3 * width), f32)]
        return call(
            functools.partial(late_kernel, groups, when, stride),
            [block()] * 3,
            scratch,
            offsets,
            outer,
            final,
            third,
            *weights,
        )

    own1, outer, final = late(1, outer, final, third)
    third = along(own1, -2, 1)
    outer = along(outer, 1, 1)
    final = along(final, 1, 1)
    own2, near, far = late(2, outer, final, third)
    near = along(near, 1, 2)
    far = along(far, 2, 2)
    (out,) = call(pick_kernel, [block()], [], own0, own1, own2, near, far)
    return out


def solution(mesh):
    placed = (P("row", "col"), P("col", None, "row", None), P())
    body = functools.partial(on_device, mesh.shape["col"], mesh.shape["row"])
    return jax.shard_map(
        body, mesh=mesh, in_specs=placed, out_specs=P("row", "col"), check_vma=False
    )
```

```python
import functools

import jax
import jax.numpy as jnp
from jax import lax
from jax.experimental import pallas as pl
from jax.experimental.pallas import tpu as pltpu
from jax.sharding import PartitionSpec as P


FACTORS = 4
TICKS = 3


def split_halves(value):
    high = value.astype(jnp.bfloat16)
    low = (value - high.astype(jnp.float32)).astype(jnp.bfloat16)
    return high, low


def product(former, high_ref, low_ref):
    rows = former.shape[0]
    high, low = split_halves(former)
    both = jnp.concatenate([high, low], 0)
    first = jnp.dot(both, high_ref[...], preferred_element_type=jnp.float32)
    second = jnp.dot(high, low_ref[...], preferred_element_type=jnp.float32)
    return first[:rows] + (first[rows:] + second)


def place(groups, offsets_ref):
    column = lax.axis_index("col")
    offset = offsets_ref[column]
    last = 2 * groups - 2 - 2 * column - offset
    return column, lax.rem(column, TICKS), offset, last


def convert(pieces, index, high_ref, low_ref):
    height = pieces[0].shape[1]
    row = lax.axis_index("row")
    for mask, piece in enumerate(pieces):
        high, low = split_halves(piece[index[mask]])
        start = pl.multiple_of((row ^ mask) * height, height)
        high_ref[pl.ds(start, height), :] = high
        low_ref[pl.ds(start, height), :] = low


def strips(first, count, stride):
    return (slice(None), pl.ds(pl.multiple_of(first * stride, stride), count * stride))


def early_kernel(groups, ring, numbers, stride, *refs):
    half = ring // 2
    refs = list(refs)
    offsets_ref = refs.pop(0)
    shift = numbers[0]
    blocks = [refs.pop(0) for _ in range(3 if shift == 0 else 1)]
    pieces = [refs.pop(0) for _ in range(ring)]
    bundled = [refs.pop(0)] if shift == 3 else []
    results = [refs.pop(0) for _ in range(2)]
    *kept, buf = refs
    _, tick, offset, last = place(groups, offsets_ref)
    active = tick == 0

    @pl.when(active)
    def _():
        width = blocks[0].shape[1]
        for i, block in enumerate(blocks):
            buf[:, i * width : (i + 1) * width] = block[...]

    for i, number in enumerate(numbers):
        index = [number] * half + [i] * half
        if shift == 0:
            convert(pieces, index, kept[2 * i], kept[2 * i + 1])

        @pl.when(active & (number <= last))
        def _():
            if shift != 0:
                convert(pieces, index, kept[2 * i], kept[2 * i + 1])
            begin = 0 if shift == 3 else offset + number - shift
            here = strips(begin, 2, stride)
            buf[here] = product(buf[here], kept[2 * i], kept[2 * i + 1])

    @pl.when(active)
    def _():
        if shift == 0:
            results[0][...] = buf[:, : 2 * stride]
            results[1][...] = buf[:, 2 * stride :]
        elif shift == 2:
            results[0][:, :stride] = buf[:, :stride]
            results[0][:, stride:] = buf[strips(3 - 2 * offset, 1, stride)]
            results[1][...] = buf[strips(1 + offset, 2, stride)]
        else:
            results[0][...] = buf[...]

    if bundled:

        @pl.when(tick == 1)
        def _():
            results[1][:1] = bundled[0][...]
            results[1][1:] = pieces[half][...]


def ready_kernel(ring, *refs):
    tick = lax.rem(lax.axis_index("col"), TICKS)
    half = ring // 2
    sets = [refs[i * ring : (i + 1) * ring] for i in range(3)]
    kept = refs[3 * ring :]

    @pl.when(tick == TICKS - 1)
    def _():
        convert(sets[0], [0] * ring, *kept[:2])
        convert(sets[0], [1] * ring, *kept[2:4])
        convert(sets[1], [2] * half + [0] * half, *kept[4:6])
        convert(sets[2], [3] * half + [0] * half, *kept[6:8])


def middle_kernel(groups, stride, *refs):
    offsets_ref, outer, final = refs[:3]
    weights = refs[3 : 3 + FACTORS]
    own, onward, buf = refs[3 + FACTORS :]
    column, tick, offset, last = place(groups, offsets_ref)
    before = offsets_ref[jnp.maximum(column - 1, 0)]

    @pl.when(tick == 1)
    def _():
        buf[:, :stride] = outer[:, :stride]
        buf[strips(3 - 2 * before, 1, stride)] = outer[:, stride:]
        buf[strips(1 + before, 2, stride)] = final[...]
        for number in range(FACTORS // 2):

            @pl.when(number <= last)
            def _():
                here = strips(offset + number, 2, stride)
                buf[here] = product(buf[here], weights[2 * number], weights[2 * number + 1])

        own[...] = buf[:, : 2 * stride]
        onward[...] = buf[:, 2 * stride :]


def last_kernel(groups, turns, stride, *refs):
    count, half = len(turns), FACTORS // 2
    offsets_ref, first, second = refs[:3]
    weights = refs[3 : 3 + 2 * count]
    *results, buf = refs[3 + 2 * count :]
    column, tick, offset, last = place(groups, offsets_ref)
    before = offsets_ref[jnp.maximum(column - 1, 0)]

    @pl.when(tick == TICKS - 1)
    def _():
        buf[:, : 2 * stride] = first[...]
        buf[:, 2 * stride :] = second[...]
        for i, turn in enumerate(turns):
            if turn < half:
                start = before + turn
                valid = turn + half <= last + 2 + offset - before
            else:
                start = offset + turn - half - (half if turns[0] else 0)
                valid = turn - half <= last

            @pl.when(valid)
            def _():
                here = strips(start, 2, stride)
                buf[here] = product(buf[here], weights[2 * i], weights[2 * i + 1])

        results[0][...] = buf[:, : 2 * stride]
        results[1][...] = buf[:, 2 * stride :]


def pick_kernel(own0, own1, own2, near, far, out):
    column = lax.axis_index("col")
    tick = lax.rem(column, TICKS)
    for source, chosen in (
        (own0, (tick == 0) & (column < TICKS)),
        (near, (tick == 0) & (column >= TICKS)),
        (own1, (tick == 1) & (column < TICKS)),
        (far, (tick == 1) & (column >= TICKS)),
        (own2, tick == 2),
    ):

        @pl.when(chosen)
        def _():
            out[...] = source[...]


def on_device(groups, ring, vectors, factors, offsets):
    rows, width = vectors.shape
    stride = width // 2
    height = factors.shape[2]
    order = ring * height
    f32, bf16 = jnp.float32, jnp.bfloat16
    on_chip = pl.BlockSpec(memory_space=pltpu.VMEM)
    scalars = pl.BlockSpec(memory_space=pltpu.SMEM)
    bits = [1 << i for i in range(ring.bit_length() - 1)]
    top = bits.pop()

    def along(array, distance, tick):
        pairs = [
            (i, i + distance)
            for i in range(groups)
            if i % TICKS == tick and 0 <= i + distance < groups
        ]
        return lax.ppermute(array, "col", pairs)

    def across(array, moves):
        pairs = [
            (row * groups + source, (row ^ top) * groups + target)
            for row in range(ring)
            for source, target in moves
        ]
        return lax.ppermute(array, ("row", "col"), pairs)

    def spread(pieces):
        for bit in bits[::-1]:
            for mask in list(pieces):
                pieces[mask ^ bit] = lax.ppermute(
                    pieces[mask], "row", [(i, i ^ bit) for i in range(ring)]
                )
        return [pieces[mask] for mask in sorted(pieces)]

    def call(kernel, outs, scratch, *operands):
        return pl.pallas_call(
            kernel,
            out_shape=outs,
            in_specs=[scalars if op.dtype == jnp.int32 else on_chip for op in operands],
            out_specs=[on_chip] * len(outs),
            scratch_shapes=scratch,
            compiler_params=pltpu.CompilerParams(vmem_limit_bytes=24 << 20),
        )(*operands)

    def block(columns=width, dtype=f32, high=rows):
        return jax.ShapeDtypeStruct((high, columns), dtype)

    def pair(count):
        return [block(order, bf16, order)] * (2 * count)

    half = FACTORS // 2
    whole = factors[0]
    same = [(i, i) for i in range(groups)]
    own = spread({0: whole})
    cuts = {0: whole[:half], 2: whole[2:3], 3: whole[3:]}
    away = {number: across(cut, same) for number, cut in cuts.items()}
    gathered = {number: own + spread({top: cut}) for number, cut in away.items()}
    handed = spread({0: along(whole[half:], 1, 1)})

    beside = along(vectors, -1, 1)
    distant = along(vectors, -2, 2)

    def early(numbers, blocks, outs, *more):
        span = sum(b.shape[1] for b in blocks)
        return call(
            functools.partial(early_kernel, groups, ring, numbers, stride),
            outs,
            ([] if blocks[1:] else [pltpu.VMEM((order, order), bf16)] * 2)
            + [pltpu.VMEM((rows, span), f32)],
            offsets,
            *blocks,
            *gathered[numbers[0]],
            *more,
        )

    own0, rest, *first_pairs = early(
        (0, 1), [vectors, beside, distant], [block(), block(2 * width), *pair(2)]
    )
    third = along(own0, -1, 0)
    outer, passing = early((2,), [rest], [block(), block()])
    outer = along(outer, 1, 0)
    bundle = jax.ShapeDtypeStruct((half, height, order), f32)
    final, bundle = early((3,), [passing], [block(), bundle], away[2])
    final = along(final, 1, 0)
    handed += spread({top: along(bundle, 1, 1)})

    second_pairs = call(
        functools.partial(ready_kernel, ring),
        pair(FACTORS),
        [],
        *handed,
        *gathered[2],
        *gathered[3],
    )
    own1, onward = call(
        functools.partial(middle_kernel, groups, stride),
        [block()] * 2,
        [pltpu.VMEM((rows, 2 * width), f32)],
        offsets,
        outer,
        final,
        *first_pairs,
    )
    onward = along(onward, 1, 1)
    fourth = along(own1, -2, 1)
    own2, near = call(
        functools.partial(last_kernel, groups, (0, 1, 2, 3), stride),
        [block()] * 2,
        [pltpu.VMEM((rows, 2 * width), f32)],
        offsets,
        onward,
        third,
        *second_pairs[: 2 * half],
        *first_pairs,
    )
    near, far = call(
        functools.partial(last_kernel, groups, (4, 5), stride),
        [block()] * 2,
        [pltpu.VMEM((rows, 2 * width), f32)],
        offsets,
        near,
        fourth,
        *second_pairs[2 * half :],
    )
    near = along(near, 1, 2)
    far = along(far, 2, 2)
    (out,) = call(pick_kernel, [block()], [], own0, own1, own2, near, far)
    return out


def solution(mesh):
    placed = (P("row", "col"), P("col", None, "row", None), P())
    ring = mesh.shape["row"]

    def body(*blocks):
        return on_device(mesh.shape["col"], ring, *blocks)

    return jax.shard_map(
        body, mesh=mesh, in_specs=placed, out_specs=P("row", "col"), check_vma=False
    )
```

```python
import functools

import jax
import jax.numpy as jnp
from jax import lax
from jax.experimental import pallas as pl
from jax.experimental.pallas import tpu as pltpu
from jax.sharding import PartitionSpec as P


FACTORS = 4
TICKS = 3


def split_halves(value):
    high = value.astype(jnp.bfloat16)
    low = (value - high.astype(jnp.float32)).astype(jnp.bfloat16)
    return high, low


def product(former, high_ref, low_ref):
    rows = former.shape[0]
    high, low = split_halves(former)
    both = jnp.concatenate([high, low], 0)
    first = jnp.dot(both, high_ref[...], preferred_element_type=jnp.float32)
    second = jnp.dot(high, low_ref[...], preferred_element_type=jnp.float32)
    return first[:rows] + (first[rows:] + second)


def place(groups, offsets_ref):
    column = lax.axis_index("col")
    offset = offsets_ref[column]
    last = 2 * groups - 2 - 2 * column - offset
    return column, lax.rem(column, TICKS), offset, last


def convert(pieces, index, high_ref, low_ref):
    height = pieces[0].shape[1]
    row = lax.axis_index("row")
    for mask, piece in enumerate(pieces):
        high, low = split_halves(piece[index[mask]])
        start = pl.multiple_of((row ^ mask) * height, height)
        high_ref[pl.ds(start, height), :] = high
        low_ref[pl.ds(start, height), :] = low


def strips(first, count, stride):
    return (slice(None), pl.ds(pl.multiple_of(first * stride, stride), count * stride))


def early_kernel(groups, ring, numbers, stride, *refs):
    half = ring // 2
    refs = list(refs)
    offsets_ref = refs.pop(0)
    shift = numbers[0]
    blocks = [refs.pop(0) for _ in range(3 if shift == 0 else 1)]
    pieces = [refs.pop(0) for _ in range(ring)]
    results = [refs.pop(0) for _ in range(1 if shift == 3 else 2)]
    *kept, buf = refs
    _, tick, offset, last = place(groups, offsets_ref)
    active = tick == 0

    @pl.when(active)
    def _():
        width = blocks[0].shape[1]
        for i, block in enumerate(blocks):
            buf[:, i * width : (i + 1) * width] = block[...]

    for i, number in enumerate(numbers):
        index = [number] * half + [i] * half
        if shift == 0:
            convert(pieces, index, kept[2 * i], kept[2 * i + 1])

        @pl.when(active & (number <= last))
        def _():
            if shift != 0:
                convert(pieces, index, kept[2 * i], kept[2 * i + 1])
            begin = 0 if shift == 3 else offset + number - shift
            here = strips(begin, 2, stride)
            buf[here] = product(buf[here], kept[2 * i], kept[2 * i + 1])

    @pl.when(active)
    def _():
        if shift == 0:
            results[0][...] = buf[:, : 2 * stride]
            results[1][...] = buf[:, 2 * stride :]
        elif shift == 2:
            results[0][:, :stride] = buf[:, :stride]
            results[0][:, stride:] = buf[strips(3 - 2 * offset, 1, stride)]
            results[1][...] = buf[strips(1 + offset, 2, stride)]
        else:
            results[0][...] = buf[...]


def ready_kernel(ring, *refs):
    tick = lax.rem(lax.axis_index("col"), TICKS)
    half = ring // 2
    kept = refs[4 * ring :]

    @pl.when(tick == TICKS - 1)
    def _():
        for i, own in enumerate((0, 1, 2, 3)):
            pieces = refs[i * ring : (i + 1) * ring]
            convert(pieces, [own] * half + [0] * half, *kept[2 * i : 2 * i + 2])


def middle_kernel(groups, stride, *refs):
    offsets_ref, outer, final = refs[:3]
    weights = refs[3 : 3 + FACTORS]
    own, onward, buf = refs[3 + FACTORS :]
    column, tick, offset, last = place(groups, offsets_ref)
    before = offsets_ref[jnp.maximum(column - 1, 0)]

    @pl.when(tick == 1)
    def _():
        buf[:, :stride] = outer[:, :stride]
        buf[strips(3 - 2 * before, 1, stride)] = outer[:, stride:]
        buf[strips(1 + before, 2, stride)] = final[...]
        for number in range(FACTORS // 2):

            @pl.when(number <= last)
            def _():
                here = strips(offset + number, 2, stride)
                buf[here] = product(buf[here], weights[2 * number], weights[2 * number + 1])

        own[...] = buf[:, : 2 * stride]
        onward[...] = buf[:, 2 * stride :]


def last_kernel(groups, turns, stride, *refs):
    count, half = len(turns), FACTORS // 2
    offsets_ref, first, second = refs[:3]
    weights = refs[3 : 3 + 2 * count]
    *results, buf = refs[3 + 2 * count :]
    column, tick, offset, last = place(groups, offsets_ref)
    before = offsets_ref[jnp.maximum(column - 1, 0)]

    @pl.when(tick == TICKS - 1)
    def _():
        buf[:, : 2 * stride] = first[...]
        buf[:, 2 * stride :] = second[...]
        for i, turn in enumerate(turns):
            if turn < half:
                start = before + turn
                valid = turn + half <= last + 2 + offset - before
            else:
                start = offset + turn - half - (half if turns[0] else 0)
                valid = turn - half <= last

            @pl.when(valid)
            def _():
                here = strips(start, 2, stride)
                buf[here] = product(buf[here], weights[2 * i], weights[2 * i + 1])

        results[0][...] = buf[:, : 2 * stride]
        results[1][...] = buf[:, 2 * stride :]


def pick_kernel(own0, own1, own2, near, far, out):
    column = lax.axis_index("col")
    tick = lax.rem(column, TICKS)
    for source, chosen in (
        (own0, (tick == 0) & (column < TICKS)),
        (near, (tick == 0) & (column >= TICKS)),
        (own1, (tick == 1) & (column < TICKS)),
        (far, (tick == 1) & (column >= TICKS)),
        (own2, tick == 2),
    ):

        @pl.when(chosen)
        def _():
            out[...] = source[...]


def on_device(groups, ring, vectors, factors, offsets):
    rows, width = vectors.shape
    stride = width // 2
    height = factors.shape[2]
    order = ring * height
    f32, bf16 = jnp.float32, jnp.bfloat16
    on_chip = pl.BlockSpec(memory_space=pltpu.VMEM)
    scalars = pl.BlockSpec(memory_space=pltpu.SMEM)
    bits = [1 << i for i in range(ring.bit_length() - 1)]
    top = bits.pop()

    def along(array, distance, tick, back="straight"):
        swaps = {
            i: i + distance
            for i in range(groups)
            if i % TICKS == tick and 0 <= i + distance < groups
        }
        moves = {i: i for i in range(groups)}
        for source, target in swaps.items():
            if back == "none":
                moves |= {source: target}
                del moves[target]
            elif back == "straight":
                moves |= {source: target, target: source}
            else:
                moves |= {source: target, target: source - 1, source - 1: source}
        pairs = [
            (row * groups + i, (row ^ 1 if i == target else row) * groups + target)
            for row in range(ring)
            for i, target in moves.items()
        ]
        return lax.ppermute(array, ("row", "col"), pairs)

    def across(array, moves):
        pairs = [
            (row * groups + source, (row ^ top) * groups + target)
            for row in range(ring)
            for source, target in moves
        ]
        return lax.ppermute(array, ("row", "col"), pairs)

    def spread(pieces):
        for bit in bits[::-1]:
            for mask in list(pieces):
                pieces[mask ^ bit] = lax.ppermute(
                    pieces[mask], "row", [(i, i ^ bit) for i in range(ring)]
                )
        return [pieces[mask] for mask in sorted(pieces)]

    def call(kernel, outs, scratch, *operands):
        return pl.pallas_call(
            kernel,
            out_shape=outs,
            in_specs=[scalars if op.dtype == jnp.int32 else on_chip for op in operands],
            out_specs=[on_chip] * len(outs),
            scratch_shapes=scratch,
            compiler_params=pltpu.CompilerParams(vmem_limit_bytes=24 << 20),
        )(*operands)

    def block(columns=width, dtype=f32, high=rows):
        return jax.ShapeDtypeStruct((high, columns), dtype)

    def pair(count):
        return [block(order, bf16, order)] * (2 * count)

    half = FACTORS // 2
    whole = factors[0]
    same = [(i, i) for i in range(groups)]
    own = spread({0: whole})
    cuts = {0: whole[:half], 2: whole[2:3], 3: whole[3:]}
    away = {number: across(cut, same) for number, cut in cuts.items()}
    gathered = {number: own + spread({top: cut}) for number, cut in away.items()}
    handed = spread({0: along(whole[half:], 1, 1, "none")})

    beside = along(vectors, -1, 1)
    distant = along(vectors, -2, 2)

    def early(numbers, blocks, outs):
        span = sum(b.shape[1] for b in blocks)
        return call(
            functools.partial(early_kernel, groups, ring, numbers, stride),
            outs,
            ([] if blocks[1:] else [pltpu.VMEM((order, order), bf16)] * 2)
            + [pltpu.VMEM((rows, span), f32)],
            offsets,
            *blocks,
            *gathered[numbers[0]],
        )

    own0, rest, *first_pairs = early(
        (0, 1), [vectors, beside, distant], [block(), block(2 * width), *pair(2)]
    )
    third = along(own0, -1, 0)
    outer, passing = early((2,), [rest], [block(), block()])
    outer = along(outer, 1, 0)
    (final,) = early((3,), [passing], [block()])
    final = along(final, 1, 0)
    passed = {
        number: spread({top: along(away[number], 1, 1, "none")})
        for number in range(half, FACTORS)
    }

    second_pairs = call(
        functools.partial(ready_kernel, ring),
        pair(FACTORS),
        [],
        *handed,
        *passed[2],
        *handed,
        *passed[3],
        *gathered[2],
        *gathered[3],
    )
    own1, onward = call(
        functools.partial(middle_kernel, groups, stride),
        [block()] * 2,
        [pltpu.VMEM((rows, 2 * width), f32)],
        offsets,
        outer,
        final,
        *first_pairs,
    )
    onward = along(onward, 1, 1, "leader")
    fourth = along(own1, -2, 1, "none")
    own2, near = call(
        functools.partial(last_kernel, groups, (0, 1, 2, 3), stride),
        [block()] * 2,
        [pltpu.VMEM((rows, 2 * width), f32)],
        offsets,
        onward,
        third,
        *second_pairs[: 2 * half],
        *first_pairs,
    )
    near, far = call(
        functools.partial(last_kernel, groups, (4, 5), stride),
        [block()] * 2,
        [pltpu.VMEM((rows, 2 * width), f32)],
        offsets,
        near,
        fourth,
        *second_pairs[2 * half :],
    )
    near = along(near, 1, 2)
    far = along(far, 2, 2)
    (out,) = call(pick_kernel, [block()], [], own0, own1, own2, near, far)
    return out


def solution(mesh):
    placed = (P("row", "col"), P("col", None, "row", None), P())
    ring = mesh.shape["row"]

    def body(*blocks):
        return on_device(mesh.shape["col"], ring, *blocks)

    return jax.shard_map(
        body, mesh=mesh, in_specs=placed, out_specs=P("row", "col"), check_vma=False
    )
```

```python
import functools

import jax
import jax.numpy as jnp
from jax import lax
from jax.experimental import pallas as pl
from jax.experimental.pallas import tpu as pltpu
from jax.sharding import PartitionSpec as P


FACTORS = 4
TICKS = 3


def split_halves(value):
    high = value.astype(jnp.bfloat16)
    low = (value - high.astype(jnp.float32)).astype(jnp.bfloat16)
    return high, low


def product(former, high_ref, low_ref):
    rows = former.shape[0]
    high, low = split_halves(former)
    both = jnp.concatenate([high, low], 0)
    first = jnp.dot(both, high_ref[...], preferred_element_type=jnp.float32)
    second = jnp.dot(high, low_ref[...], preferred_element_type=jnp.float32)
    return first[:rows] + (first[rows:] + second)


def place(groups, offsets_ref):
    column = lax.axis_index("col")
    offset = offsets_ref[column]
    last = 2 * groups - 2 - 2 * column - offset
    return column, lax.rem(column, TICKS), offset, last


def convert(pieces, index, high_ref, low_ref):
    height = pieces[0].shape[1]
    row = lax.axis_index("row")
    for mask, piece in enumerate(pieces):
        high, low = split_halves(piece[index[mask]])
        start = pl.multiple_of((row ^ mask) * height, height)
        high_ref[pl.ds(start, height), :] = high
        low_ref[pl.ds(start, height), :] = low


def strips(first, count, stride):
    return (slice(None), pl.ds(pl.multiple_of(first * stride, stride), count * stride))


def early_kernel(groups, ring, numbers, stride, *refs):
    half = ring // 2
    refs = list(refs)
    offsets_ref = refs.pop(0)
    shift = numbers[0]
    blocks = [refs.pop(0) for _ in range(3 if shift == 0 else 1)]
    pieces = [refs.pop(0) for _ in range(ring)]
    results = [refs.pop(0) for _ in range(3 if shift == 0 else 2)]
    *kept, buf = refs
    _, tick, offset, last = place(groups, offsets_ref)
    active = tick == 0

    @pl.when(active)
    def _():
        width = blocks[0].shape[1]
        for i, block in enumerate(blocks):
            buf[:, i * width : (i + 1) * width] = block[...]

    for i, number in enumerate(numbers):
        index = [number] * half + [i] * half
        if shift == 0:
            convert(pieces, index, kept[2 * i], kept[2 * i + 1])

        @pl.when(active & (number <= last))
        def _():
            if shift != 0:
                convert(pieces, index, kept[2 * i], kept[2 * i + 1])
            begin = 0 if shift == 3 else offset + number - shift
            here = strips(begin, 2, stride)
            buf[here] = product(buf[here], kept[2 * i], kept[2 * i + 1])

    @pl.when(active)
    def _():
        if shift == 0:
            results[0][...] = buf[:, : 2 * stride]
            results[1][...] = buf[:, 2 * stride :]
            results[2][...] = buf[strips(5 - 3 * offset, 1, stride)]
        elif shift == 2:
            results[0][...] = buf[strips(offset, 1, stride)]
            results[1][...] = buf[strips(1 + offset, 2, stride)]
        else:
            upper = buf.shape[0] // 2
            results[0][...] = buf[:upper]
            results[1][...] = buf[upper:]


def ready_kernel(ring, numbers, *refs):
    tick = lax.rem(lax.axis_index("col"), TICKS)
    half = ring // 2
    kept = refs[len(numbers) * ring :]

    @pl.when(tick == TICKS - 1)
    def _():
        for i, (near, away) in enumerate(numbers):
            pieces = refs[i * ring : (i + 1) * ring]
            convert(pieces, [near] * half + [away] * half, *kept[2 * i : 2 * i + 2])


def middle_kernel(groups, part, stride, *refs):
    offsets_ref, ahead, outer, final = refs[:4]
    weights = refs[4 : 4 + FACTORS]
    own, onward, buf = refs[4 + FACTORS :]
    column, tick, offset, last = place(groups, offsets_ref)
    before = offsets_ref[jnp.maximum(column - 1, 0)]

    height = buf.shape[0]

    @pl.when(tick == 1)
    def _():
        these = slice(part * height, (part + 1) * height)
        buf[strips(3 - 3 * before, 1, stride)] = ahead[these]
        buf[strips(before, 1, stride)] = outer[these]
        buf[strips(1 + before, 2, stride)] = final[...]
        for number in range(FACTORS // 2):

            @pl.when(number <= last)
            def _():
                here = strips(offset + number, 2, stride)
                buf[here] = product(buf[here], weights[2 * number], weights[2 * number + 1])

        own[...] = buf[:, : 2 * stride]
        onward[...] = buf[:, 2 * stride :]


def last_kernel(groups, part, turns, stride, *refs):
    count, half = len(turns), FACTORS // 2
    offsets_ref, first, second = refs[:3]
    weights = refs[3 : 3 + 2 * count]
    *results, buf = refs[3 + 2 * count :]
    column, tick, offset, last = place(groups, offsets_ref)
    before = offsets_ref[jnp.maximum(column - 1, 0)]

    height = buf.shape[0]

    @pl.when(tick == TICKS - 1)
    def _():
        buf[:, : 2 * stride] = first[...]
        if second.shape[0] == height:
            buf[:, 2 * stride :] = second[...]
        else:
            buf[:, 2 * stride :] = second[part * height : (part + 1) * height]
        for i, turn in enumerate(turns):
            if turn < half:
                start = before + turn
                valid = turn + half <= last + 2 + offset - before
            else:
                start = offset + turn - half - (half if turns[0] else 0)
                valid = turn - half <= last

            @pl.when(valid)
            def _():
                here = strips(start, 2, stride)
                buf[here] = product(buf[here], weights[2 * i], weights[2 * i + 1])

        results[0][...] = buf[:, : 2 * stride]
        results[1][...] = buf[:, 2 * stride :]


def pick_kernel(own0, *refs):
    *sources, out = refs
    column = lax.axis_index("col")
    tick = lax.rem(column, TICKS)
    height = out.shape[0] // 2

    @pl.when((tick == 0) & (column < TICKS))
    def _():
        out[...] = own0[...]

    for i, chosen in enumerate(
        (
            (tick == 1) & (column < TICKS),
            tick == 2,
            (tick == 0) & (column >= TICKS),
            (tick == 1) & (column >= TICKS),
        )
    ):

        @pl.when(chosen)
        def _():
            out[:height] = sources[2 * i][...]
            out[height:] = sources[2 * i + 1][...]


def on_device(groups, ring, vectors, factors, offsets):
    rows, width = vectors.shape
    stride = width // 2
    height = factors.shape[2]
    order = ring * height
    f32, bf16 = jnp.float32, jnp.bfloat16
    on_chip = pl.BlockSpec(memory_space=pltpu.VMEM)
    scalars = pl.BlockSpec(memory_space=pltpu.SMEM)
    bits = [1 << i for i in range(ring.bit_length() - 1)]
    top = bits.pop()

    def along(array, distance, tick, back=True):
        swaps = {
            i: i + distance
            for i in range(groups)
            if i % TICKS == tick and 0 <= i + distance < groups
        }
        moves = {i: i for i in range(groups)}
        for source, target in swaps.items():
            moves |= {source: target, target: source}
        if not back:
            for target in swaps.values():
                del moves[target]
        pairs = [
            (row * groups + i, (row ^ 1 if i == target else row) * groups + target)
            for row in range(ring)
            for i, target in moves.items()
        ]
        return lax.ppermute(array, ("row", "col"), pairs)

    def across(array, ticks):
        pairs = [
            (row * groups + i, (row ^ (top if i % TICKS in ticks else 1)) * groups + i)
            for row in range(ring)
            for i in range(groups)
        ]
        return lax.ppermute(array, ("row", "col"), pairs)

    def spread(pieces):
        for bit in bits[::-1]:
            for mask in list(pieces):
                pieces[mask ^ bit] = lax.ppermute(
                    pieces[mask], "row", [(i, i ^ bit) for i in range(ring)]
                )
        return [pieces[mask] for mask in sorted(pieces)]

    def call(kernel, outs, scratch, *operands):
        return pl.pallas_call(
            kernel,
            out_shape=outs,
            in_specs=[scalars if op.dtype == jnp.int32 else on_chip for op in operands],
            out_specs=[on_chip] * len(outs),
            scratch_shapes=scratch,
            compiler_params=pltpu.CompilerParams(vmem_limit_bytes=24 << 20),
        )(*operands)

    def block(columns=width, dtype=f32, high=rows):
        return jax.ShapeDtypeStruct((high, columns), dtype)

    def pair(count):
        return [block(order, bf16, order)] * (2 * count)

    half = FACTORS // 2
    whole = factors[0]
    own = spread({0: whole})
    away = {
        0: across(whole[:half], (0, 1, 2)),
        2: across(whole[2:3], (0, 2)),
        3: across(whole[3:], (0,)),
    }
    gathered = {number: own + spread({top: cut}) for number, cut in away.items()}
    handed = along(whole[half:], 1, 1, False)
    crossed = across(handed, (2,))
    handed = spread({0: handed}) + spread({top: crossed})
    mine = own + spread({top: across(whole[3:], (2,))})

    beside = along(vectors, -1, 1)
    distant = along(vectors, -2, 2)

    def early(numbers, blocks, outs):
        span = sum(b.shape[1] for b in blocks)
        return call(
            functools.partial(early_kernel, groups, ring, numbers, stride),
            outs,
            ([] if blocks[1:] else [pltpu.VMEM((order, order), bf16)] * 2)
            + [pltpu.VMEM((rows, span), f32)],
            offsets,
            *blocks,
            *gathered[numbers[0]],
        )

    own0, rest, ahead, *first_pairs = early(
        (0, 1), [vectors, beside, distant], [block(), block(2 * width), block(stride), *pair(2)]
    )
    ahead = along(ahead, 1, 0)
    third = along(own0, -1, 0, False)
    outer, passing = early((2,), [rest], [block(stride), block()])
    outer = along(outer, 1, 0)
    final = early((3,), [passing], [block(high=rows // 2)] * 2)
    final = [along(part, 1, 0) for part in final]

    def ready(numbers, *pieces):
        return call(functools.partial(ready_kernel, ring, numbers), pair(len(numbers)), [], *pieces)

    handed_pairs = ready(((0, 0), (1, 1)), *handed, *handed)
    last_pairs = ready(((2, 0), (3, 0)), *gathered[2], *mine)
    low = block(high=rows // 2)
    buf = pltpu.VMEM((rows // 2, 2 * width), f32)
    own1, onward, fourth, own2, near, far = [], [], [], [], [], []
    for i in range(2):
        kept, sent = call(
            functools.partial(middle_kernel, groups, i, stride),
            [low] * 2,
            [buf],
            offsets,
            ahead,
            outer,
            final[i],
            *first_pairs,
        )
        own1.append(kept)
        onward.append(along(sent, 1, 1))
        fourth.append(along(kept, -2, 1))
    for i in range(2):
        kept, sent = call(
            functools.partial(last_kernel, groups, i, (0, 1, 2, 3), stride),
            [low] * 2,
            [buf],
            offsets,
            onward[i],
            third,
            *handed_pairs,
            *first_pairs,
        )
        own2.append(kept)
        next_block, after = call(
            functools.partial(last_kernel, groups, i, (4, 5), stride),
            [low] * 2,
            [buf],
            offsets,
            sent,
            fourth[i],
            *last_pairs,
        )
        near.append(along(next_block, 1, 2))
        far.append(along(after, 2, 2))
    (out,) = call(pick_kernel, [block()], [], own0, *own1, *own2, *near, *far)
    return out


def solution(mesh):
    placed = (P("row", "col"), P("col", None, "row", None), P())
    ring = mesh.shape["row"]

    def body(*blocks):
        return on_device(mesh.shape["col"], ring, *blocks)

    return jax.shard_map(
        body, mesh=mesh, in_specs=placed, out_specs=P("row", "col"), check_vma=False
    )
```

```python
import functools

import jax
import jax.numpy as jnp
from jax import lax
from jax.experimental import pallas as pl
from jax.experimental.pallas import tpu as pltpu
from jax.sharding import PartitionSpec as P


FACTORS = 4
TICKS = 3


def split_halves(value):
    high = value.astype(jnp.bfloat16)
    low = (value - high.astype(jnp.float32)).astype(jnp.bfloat16)
    return high, low


def product(former, high_ref, low_ref):
    rows = former.shape[0]
    high, low = split_halves(former)
    both = jnp.concatenate([high, low], 0)
    first = jnp.dot(both, high_ref[...], preferred_element_type=jnp.float32)
    second = jnp.dot(high, low_ref[...], preferred_element_type=jnp.float32)
    return first[:rows] + (first[rows:] + second)


def place(groups, offsets_ref):
    column = lax.axis_index("col")
    offset = offsets_ref[column]
    last = 2 * groups - 2 - 2 * column - offset
    return column, lax.rem(column, TICKS), offset, last


def convert(pieces, index, high_ref, low_ref):
    height = pieces[0].shape[1]
    row = lax.axis_index("row")
    for mask, piece in enumerate(pieces):
        high, low = split_halves(piece[index[mask]])
        start = pl.multiple_of((row ^ mask) * height, height)
        high_ref[pl.ds(start, height), :] = high
        low_ref[pl.ds(start, height), :] = low


def strips(first, count, stride):
    return (slice(None), pl.ds(pl.multiple_of(first * stride, stride), count * stride))


def early_kernel(groups, ring, numbers, stride, *refs):
    half = ring // 2
    refs = list(refs)
    offsets_ref = refs.pop(0)
    shift = numbers[0]
    blocks = [refs.pop(0) for _ in range(3 if shift == 0 else 1)]
    pieces = [refs.pop(0) for _ in range(ring)]
    results = [refs.pop(0) for _ in range(3 if shift == 0 else 2)]
    *kept, buf = refs
    _, tick, offset, last = place(groups, offsets_ref)
    active = tick == 0

    @pl.when(active)
    def _():
        width = blocks[0].shape[1]
        for i, block in enumerate(blocks):
            buf[:, i * width : (i + 1) * width] = block[...]

    for i, number in enumerate(numbers):
        index = [number] * half + [i] * half
        if shift == 0:
            convert(pieces, index, kept[2 * i], kept[2 * i + 1])

        @pl.when(active & (number <= last))
        def _():
            if shift != 0:
                convert(pieces, index, kept[2 * i], kept[2 * i + 1])
            begin = 0 if shift == 3 else offset + number - shift
            here = strips(begin, 2, stride)
            buf[here] = product(buf[here], kept[2 * i], kept[2 * i + 1])

    @pl.when(active)
    def _():
        if shift == 0:
            results[0][...] = buf[:, : 2 * stride]
            results[1][...] = buf[:, 2 * stride :]
            results[2][...] = buf[strips(5 - 3 * offset, 1, stride)]
        elif shift == 2:
            results[0][...] = buf[strips(offset, 1, stride)]
            results[1][...] = buf[strips(1 + offset, 2, stride)]
        else:
            upper = buf.shape[0] // 2
            results[0][...] = buf[:upper]
            results[1][...] = buf[upper:]


def ready_kernel(ring, numbers, *refs):
    tick = lax.rem(lax.axis_index("col"), TICKS)
    half = ring // 2
    kept = refs[len(numbers) * ring :]

    @pl.when(tick == TICKS - 1)
    def _():
        for i, (near, away) in enumerate(numbers):
            pieces = refs[i * ring : (i + 1) * ring]
            convert(pieces, [near] * half + [away] * half, *kept[2 * i : 2 * i + 2])


def middle_kernel(groups, part, stride, *refs):
    offsets_ref, ahead, outer, final = refs[:4]
    weights = refs[4 : 4 + FACTORS]
    own, onward, buf = refs[4 + FACTORS :]
    column, tick, offset, last = place(groups, offsets_ref)
    before = offsets_ref[jnp.maximum(column - 1, 0)]

    height = buf.shape[0]

    @pl.when(tick == 1)
    def _():
        these = slice(part * height, (part + 1) * height)
        buf[strips(3 - 3 * before, 1, stride)] = ahead[these]
        buf[strips(before, 1, stride)] = outer[these]
        buf[strips(1 + before, 2, stride)] = final[...]
        for number in range(FACTORS // 2):

            @pl.when(number <= last)
            def _():
                here = strips(offset + number, 2, stride)
                buf[here] = product(buf[here], weights[2 * number], weights[2 * number + 1])

        own[...] = buf[:, : 2 * stride]
        onward[...] = buf[:, 2 * stride :]


def last_kernel(groups, part, turns, stride, *refs):
    count, half = len(turns), FACTORS // 2
    places = 3 if count == FACTORS + half else 2
    offsets_ref, *blocks = refs[: 1 + places]
    weights = refs[1 + places : 1 + places + 2 * count]
    *results, buf = refs[1 + places + 2 * count :]
    column, tick, offset, last = place(groups, offsets_ref)
    before = offsets_ref[jnp.maximum(column - 1, 0)]

    height = buf.shape[0]

    @pl.when(tick == TICKS - 1)
    def _():
        for i, block in enumerate(blocks):
            first = part * height if block.shape[0] > height else 0
            buf[:, 2 * i * stride : 2 * (i + 1) * stride] = block[first : first + height]
        for i, turn in enumerate(turns):
            if turn < half:
                start = before + turn
                valid = turn + half <= last + 2 + offset - before
            else:
                start = offset + turn - half - (half if turns[0] else 0)
                valid = turn - half <= last

            @pl.when(valid)
            def _():
                here = strips(start, 2, stride)
                buf[here] = product(buf[here], weights[2 * i], weights[2 * i + 1])

        for i, result in enumerate(results):
            result[...] = buf[:, 2 * i * stride : 2 * (i + 1) * stride]


def pick_kernel(own0, *refs):
    *sources, out = refs
    column = lax.axis_index("col")
    tick = lax.rem(column, TICKS)
    height = out.shape[0] // 2

    @pl.when((tick == 0) & (column < TICKS))
    def _():
        out[...] = own0[...]

    for i, chosen in enumerate(
        (
            (tick == 1) & (column < TICKS),
            tick == 2,
            (tick == 0) & (column >= TICKS) & (lax.rem(column, 2) == 1),
            (tick == 0) & (column >= TICKS) & (lax.rem(column, 2) == 0),
            (tick == 1) & (column >= TICKS),
        )
    ):

        @pl.when(chosen)
        def _():
            out[:height] = sources[2 * i][...]
            out[height:] = sources[2 * i + 1][...]


def on_device(groups, ring, vectors, factors, offsets):
    rows, width = vectors.shape
    stride = width // 2
    height = factors.shape[2]
    order = ring * height
    f32, bf16 = jnp.float32, jnp.bfloat16
    on_chip = pl.BlockSpec(memory_space=pltpu.VMEM)
    scalars = pl.BlockSpec(memory_space=pltpu.SMEM)
    bits = [1 << i for i in range(ring.bit_length() - 1)]
    top = bits.pop()

    def along(array, distance, tick, back=True):
        swaps = {
            i: i + distance
            for i in range(groups)
            if i % TICKS == tick and 0 <= i + distance < groups
        }
        return trade(array, swaps, back)

    def trade(array, swaps, back=True):
        moves = {i: i for i in range(groups)}
        for source, target in swaps.items():
            moves |= {source: target, target: source}
        if not back:
            for target in swaps.values():
                del moves[target]
        pairs = [
            (row * groups + i, (row ^ 1 if i == target else row) * groups + target)
            for row in range(ring)
            for i, target in moves.items()
        ]
        return lax.ppermute(array, ("row", "col"), pairs)

    def across(array, ticks):
        pairs = [
            (row * groups + i, (row ^ (top if i % TICKS in ticks else 1)) * groups + i)
            for row in range(ring)
            for i in range(groups)
        ]
        return lax.ppermute(array, ("row", "col"), pairs)

    def spread(pieces):
        for bit in bits[::-1]:
            for mask in list(pieces):
                pieces[mask ^ bit] = lax.ppermute(
                    pieces[mask], "row", [(i, i ^ bit) for i in range(ring)]
                )
        return [pieces[mask] for mask in sorted(pieces)]

    def call(kernel, outs, scratch, *operands):
        return pl.pallas_call(
            kernel,
            out_shape=outs,
            in_specs=[scalars if op.dtype == jnp.int32 else on_chip for op in operands],
            out_specs=[on_chip] * len(outs),
            scratch_shapes=scratch,
            compiler_params=pltpu.CompilerParams(vmem_limit_bytes=24 << 20),
        )(*operands)

    def block(columns=width, dtype=f32, high=rows):
        return jax.ShapeDtypeStruct((high, columns), dtype)

    def pair(count):
        return [block(order, bf16, order)] * (2 * count)

    half = FACTORS // 2
    kinds = [[i for i in range(groups) if i % TICKS == tick] for tick in range(TICKS)]
    whole = factors[0]
    own = spread({0: whole})
    away = {
        0: across(whole[:half], (0, 1, 2)),
        2: across(whole[2:3], (0, 2)),
        3: across(whole[3:], (0,)),
    }
    gathered = {number: own + spread({top: cut}) for number, cut in away.items()}
    handed = along(whole[half:], 1, 1, False)
    crossed = across(handed, (2,))
    handed = spread({0: handed}) + spread({top: crossed})
    mine = own + spread({top: across(whole[3:], (2,))})

    beside = along(vectors, -1, 1)
    distant = along(vectors, -2, 2)

    def early(numbers, blocks, outs):
        span = sum(b.shape[1] for b in blocks)
        return call(
            functools.partial(early_kernel, groups, ring, numbers, stride),
            outs,
            ([] if blocks[1:] else [pltpu.VMEM((order, order), bf16)] * 2)
            + [pltpu.VMEM((rows, span), f32)],
            offsets,
            *blocks,
            *gathered[numbers[0]],
        )

    own0, rest, ahead, *first_pairs = early(
        (0, 1), [vectors, beside, distant], [block(), block(2 * width), block(stride), *pair(2)]
    )
    ahead = along(ahead, 1, 0)
    third = along(own0, -1, 0, False)
    outer, passing = early((2,), [rest], [block(stride), block()])
    outer = along(outer, 1, 0)
    final = early((3,), [passing], [block(high=rows // 2)] * 2)
    final = [along(part, 1, 0) for part in final]

    def ready(numbers, *pieces):
        return call(functools.partial(ready_kernel, ring, numbers), pair(len(numbers)), [], *pieces)

    handed_pairs = ready(((0, 0), (1, 1)), *handed, *handed)
    last_pairs = ready(((2, 0), (3, 0)), *gathered[2], *mine)
    low = block(high=rows // 2)
    buf = pltpu.VMEM((rows // 2, 2 * width), f32)
    own1, onward, fourth = [], [], []
    for i in range(2):
        kept, sent = call(
            functools.partial(middle_kernel, groups, i, stride),
            [low] * 2,
            [buf],
            offsets,
            ahead,
            outer,
            final[i],
            *first_pairs,
        )
        own1.append(kept)
        onward.append(along(sent, 1, 1))
        fourth.append(along(kept, -2, 1))

    def finish(part, turns, blocks, weights):
        return call(
            functools.partial(last_kernel, groups, part, turns, stride),
            [low] * len(blocks),
            [pltpu.VMEM((rows // 2, len(blocks) * width), f32)],
            offsets,
            *blocks,
            *weights,
        )

    early_turns = [*handed_pairs, *first_pairs]
    kept, sent = finish(0, (0, 1, 2, 3), [onward[0], third], early_turns)
    own2 = [kept]
    near, far = finish(0, (4, 5), [sent, fourth[0]], last_pairs)
    lasts = [i for i in kinds[2] if i + 1 < groups]
    near0 = trade(near, {i: i - 1 if i % 2 else i + 1 for i in lasts})
    far0 = along(far, 2, 2)
    kept, near, far = finish(
        1, (0, 1, 2, 3, 4, 5), [onward[1], third, fourth[1]], early_turns + list(last_pairs)
    )
    own2.append(kept)
    near1 = along(near, 1, 2)
    far1 = along(far, 2, 2)
    relayed = trade(near0, {i - 1: i + 1 for i in lasts if i % 2}, False)
    (out,) = call(
        pick_kernel, [block()], [], own0, *own1, *own2, near0, near1, relayed, near1, far0, far1
    )
    return out


def solution(mesh):
    placed = (P("row", "col"), P("col", None, "row", None), P())
    ring = mesh.shape["row"]

    def body(*blocks):
        return on_device(mesh.shape["col"], ring, *blocks)

    return jax.shard_map(
        body, mesh=mesh, in_specs=placed, out_specs=P("row", "col"), check_vma=False
    )
```

```python
import functools

import jax
import jax.numpy as jnp
from jax import lax
from jax.experimental import pallas as pl
from jax.experimental.pallas import tpu as pltpu
from jax.sharding import PartitionSpec as P


FACTORS = 4
TICKS = 3


def split_halves(value):
    high = value.astype(jnp.bfloat16)
    low = (value - high.astype(jnp.float32)).astype(jnp.bfloat16)
    return high, low


def product(former, high_ref, low_ref):
    rows = former.shape[0]
    high, low = split_halves(former)
    both = jnp.concatenate([high, low], 0)
    first = jnp.dot(both, high_ref[...], preferred_element_type=jnp.float32)
    second = jnp.dot(high, low_ref[...], preferred_element_type=jnp.float32)
    return first[:rows] + (first[rows:] + second)


def place(groups, offsets_ref):
    column = lax.axis_index("col")
    offset = offsets_ref[column]
    last = 2 * groups - 2 - 2 * column - offset
    return column, lax.rem(column, TICKS), offset, last


def convert(pieces, index, high_ref, low_ref):
    height = pieces[0].shape[1]
    row = lax.axis_index("row")
    for mask, piece in enumerate(pieces):
        high, low = split_halves(piece[index[mask]])
        start = pl.multiple_of((row ^ mask) * height, height)
        high_ref[pl.ds(start, height), :] = high
        low_ref[pl.ds(start, height), :] = low


def strips(first, count, stride):
    return (slice(None), pl.ds(pl.multiple_of(first * stride, stride), count * stride))


def early_kernel(groups, ring, numbers, stride, *refs):
    half = ring // 2
    refs = list(refs)
    offsets_ref = refs.pop(0)
    shift = numbers[0]
    blocks = [refs.pop(0) for _ in range(3 if shift == 0 else 1)]
    pieces = [refs.pop(0) for _ in range(ring)]
    results = [refs.pop(0) for _ in range(3 if shift == 0 else 2)]
    *kept, buf = refs
    _, tick, offset, last = place(groups, offsets_ref)
    active = tick == 0

    @pl.when(active)
    def _():
        width = blocks[0].shape[1]
        for i, block in enumerate(blocks):
            buf[:, i * width : (i + 1) * width] = block[...]

    for i, number in enumerate(numbers):
        index = [number] * half + [i] * half
        if shift == 0:
            convert(pieces, index, kept[2 * i], kept[2 * i + 1])

        @pl.when(active & (number <= last))
        def _():
            if shift != 0:
                convert(pieces, index, kept[2 * i], kept[2 * i + 1])
            begin = 0 if shift == 3 else offset + number - shift
            here = strips(begin, 2, stride)
            buf[here] = product(buf[here], kept[2 * i], kept[2 * i + 1])

    @pl.when(active)
    def _():
        if shift == 0:
            results[0][...] = buf[:, : 2 * stride]
            results[1][...] = buf[:, 2 * stride :]
            results[2][...] = buf[strips(5 - 3 * offset, 1, stride)]
        elif shift == 2:
            results[0][...] = buf[strips(offset, 1, stride)]
            results[1][...] = buf[strips(1 + offset, 2, stride)]
        else:
            upper = buf.shape[0] // 2
            results[0][...] = buf[:upper]
            results[1][...] = buf[upper:]


def ready_kernel(ring, numbers, *refs):
    tick = lax.rem(lax.axis_index("col"), TICKS)
    half = ring // 2
    kept = refs[len(numbers) * ring :]

    @pl.when(tick == TICKS - 1)
    def _():
        for i, (near, away) in enumerate(numbers):
            pieces = refs[i * ring : (i + 1) * ring]
            convert(pieces, [near] * half + [away] * half, *kept[2 * i : 2 * i + 2])


def middle_kernel(groups, part, stride, *refs):
    offsets_ref, ahead, outer, final = refs[:4]
    weights = refs[4 : 4 + FACTORS]
    own, onward, buf = refs[4 + FACTORS :]
    column, tick, offset, last = place(groups, offsets_ref)
    before = offsets_ref[jnp.maximum(column - 1, 0)]

    height = buf.shape[0]

    @pl.when(tick == 1)
    def _():
        these = slice(part * height, (part + 1) * height)
        buf[strips(3 - 3 * before, 1, stride)] = ahead[these]
        buf[strips(before, 1, stride)] = outer[these]
        buf[strips(1 + before, 2, stride)] = final[...]
        for number in range(FACTORS // 2):

            @pl.when(number <= last)
            def _():
                here = strips(offset + number, 2, stride)
                buf[here] = product(buf[here], weights[2 * number], weights[2 * number + 1])

        own[...] = buf[:, : 2 * stride]
        onward[...] = buf[:, 2 * stride :]


def last_kernel(groups, part, turns, stride, *refs):
    count, half = len(turns), FACTORS // 2
    places = 3 if count == FACTORS + half else 2
    offsets_ref, *blocks = refs[: 1 + places]
    weights = refs[1 + places : 1 + places + 2 * count]
    *results, buf = refs[1 + places + 2 * count :]
    column, tick, offset, last = place(groups, offsets_ref)
    before = offsets_ref[jnp.maximum(column - 1, 0)]

    height = buf.shape[0]

    @pl.when(tick == TICKS - 1)
    def _():
        for i, block in enumerate(blocks):
            first = part * height if block.shape[0] > height else 0
            buf[:, 2 * i * stride : 2 * (i + 1) * stride] = block[first : first + height]
        for i, turn in enumerate(turns):
            if turn < half:
                start = before + turn
                valid = turn + half <= last + 2 + offset - before
            else:
                start = offset + turn - half - (half if turns[0] else 0)
                valid = turn - half <= last

            @pl.when(valid)
            def _():
                here = strips(start, 2, stride)
                buf[here] = product(buf[here], weights[2 * i], weights[2 * i + 1])

        for i, result in enumerate(results):
            result[...] = buf[:, 2 * i * stride : 2 * (i + 1) * stride]


def pick_kernel(own0, *refs):
    *sources, out = refs
    column = lax.axis_index("col")
    tick = lax.rem(column, TICKS)
    height = out.shape[0] // 2

    @pl.when((tick == 0) & (column < TICKS))
    def _():
        out[...] = own0[...]

    for i, chosen in enumerate(
        (
            (tick == 1) & (column < TICKS),
            tick == 2,
            (tick == 0) & (column >= TICKS) & (lax.rem(column, 2) == 1),
            (tick == 0) & (column >= TICKS) & (lax.rem(column, 2) == 0),
            (tick == 1) & (column >= TICKS),
        )
    ):

        @pl.when(chosen)
        def _():
            out[:height] = sources[2 * i][...]
            out[height:] = sources[2 * i + 1][...]


def on_device(groups, ring, vectors, factors, offsets):
    rows, width = vectors.shape
    stride = width // 2
    height = factors.shape[2]
    order = ring * height
    f32, bf16 = jnp.float32, jnp.bfloat16
    on_chip = pl.BlockSpec(memory_space=pltpu.VMEM)
    scalars = pl.BlockSpec(memory_space=pltpu.SMEM)
    bits = [1 << i for i in range(ring.bit_length() - 1)]
    top = bits.pop()

    def along(array, distance, tick, back=True):
        swaps = {
            i: i + distance
            for i in range(groups)
            if i % TICKS == tick and 0 <= i + distance < groups
        }
        return trade(array, swaps, back)

    def trade(array, swaps, back=True):
        moves = {i: i for i in range(groups)}
        for source, target in swaps.items():
            moves |= {source: target, target: source}
        if not back:
            for target in swaps.values():
                del moves[target]
        pairs = [
            (row * groups + i, (row ^ 1 if i == target else row) * groups + target)
            for row in range(ring)
            for i, target in moves.items()
        ]
        return lax.ppermute(array, ("row", "col"), pairs)

    def across(array, ticks):
        pairs = [
            (row * groups + i, (row ^ (top if i % TICKS in ticks else 1)) * groups + i)
            for row in range(ring)
            for i in range(groups)
        ]
        return lax.ppermute(array, ("row", "col"), pairs)

    def spread(pieces):
        for bit in bits[::-1]:
            for mask in list(pieces):
                pieces[mask ^ bit] = lax.ppermute(
                    pieces[mask], "row", [(i, i ^ bit) for i in range(ring)]
                )
        return [pieces[mask] for mask in sorted(pieces)]

    def call(kernel, outs, scratch, *operands):
        return pl.pallas_call(
            kernel,
            out_shape=outs,
            in_specs=[scalars if op.dtype == jnp.int32 else on_chip for op in operands],
            out_specs=[on_chip] * len(outs),
            scratch_shapes=scratch,
            compiler_params=pltpu.CompilerParams(vmem_limit_bytes=24 << 20),
        )(*operands)

    def block(columns=width, dtype=f32, high=rows):
        return jax.ShapeDtypeStruct((high, columns), dtype)

    def pair(count):
        return [block(order, bf16, order)] * (2 * count)

    half = FACTORS // 2
    kinds = [[i for i in range(groups) if i % TICKS == tick] for tick in range(TICKS)]
    whole = factors[0]
    own = spread({0: whole})
    away = {
        0: across(whole[:half], (0, 1, 2)),
        2: across(whole[2:3], (0, 2)),
        3: across(whole[3:], (0,)),
    }
    gathered = {number: own + spread({top: cut}) for number, cut in away.items()}
    handed = along(whole[half:], 1, 1, False)
    crossed = across(handed, (2,))
    handed = spread({0: handed}) + spread({top: crossed})
    mine = own + spread({top: across(whole[3:], (2,))})

    beside = along(vectors, -1, 1)
    distant = along(vectors, -2, 2)

    def early(numbers, blocks, outs):
        span = sum(b.shape[1] for b in blocks)
        return call(
            functools.partial(early_kernel, groups, ring, numbers, stride),
            outs,
            ([] if blocks[1:] else [pltpu.VMEM((order, order), bf16)] * 2)
            + [pltpu.VMEM((rows, span), f32)],
            offsets,
            *blocks,
            *gathered[numbers[0]],
        )

    own0, rest, ahead, *first_pairs = early(
        (0, 1), [vectors, beside, distant], [block(), block(2 * width), block(stride), *pair(2)]
    )
    ahead = along(ahead, 1, 0)
    third = along(own0, -1, 0, False)
    outer, passing = early((2,), [rest], [block(stride), block()])
    outer = along(outer, 1, 0)
    final = early((3,), [passing], [block(high=rows // 2)] * 2)
    final = [along(part, 1, 0) for part in final]

    def ready(numbers, *pieces):
        return call(functools.partial(ready_kernel, ring, numbers), pair(len(numbers)), [], *pieces)

    handed_pairs = ready(((0, 0), (1, 1), (2, 0)), *handed, *handed, *gathered[2])
    last_pairs = [*handed_pairs[4:], *ready(((3, 0),), *mine)]
    handed_pairs = handed_pairs[:4]
    low = block(high=rows // 2)
    buf = pltpu.VMEM((rows // 2, 2 * width), f32)
    own1, onward, fourth = [], [], []
    for i in range(2):
        kept, sent = call(
            functools.partial(middle_kernel, groups, i, stride),
            [low] * 2,
            [buf],
            offsets,
            ahead,
            outer,
            final[i],
            *first_pairs,
        )
        own1.append(kept)
        onward.append(along(sent, 1, 1))
        fourth.append(along(kept, -2, 1))

    def finish(part, turns, blocks, weights):
        return call(
            functools.partial(last_kernel, groups, part, turns, stride),
            [low] * len(blocks),
            [pltpu.VMEM((rows // 2, len(blocks) * width), f32)],
            offsets,
            *blocks,
            *weights,
        )

    early_turns = [*handed_pairs, *first_pairs]
    kept, sent = finish(0, (0, 1, 2, 3), [onward[0], third], early_turns)
    own2 = [kept]
    near, far = finish(0, (4, 5), [sent, fourth[0]], last_pairs)
    lasts = [i for i in kinds[2] if i + 1 < groups]
    near0 = trade(near, {i: i - 1 if i % 2 else i + 1 for i in lasts})
    far0 = along(far, 2, 2)
    kept, near, far = finish(
        1, (0, 1, 2, 3, 4, 5), [onward[1], third, fourth[1]], early_turns + list(last_pairs)
    )
    own2.append(kept)
    near1 = along(near, 1, 2)
    far1 = along(far, 2, 2)
    relayed = trade(near0, {i - 1: i + 1 for i in lasts if i % 2}, False)
    (out,) = call(
        pick_kernel, [block()], [], own0, *own1, *own2, near0, near1, relayed, near1, far0, far1
    )
    return out


def solution(mesh):
    placed = (P("row", "col"), P("col", None, "row", None), P())
    ring = mesh.shape["row"]

    def body(*blocks):
        return on_device(mesh.shape["col"], ring, *blocks)

    return jax.shard_map(
        body, mesh=mesh, in_specs=placed, out_specs=P("row", "col"), check_vma=False
    )
```
